256 devices in a mesh: seq: 64 (over z, y, core), pool: 4 (over x).
Axes of the slice: x: 4, y: 4, z: 8, core: 2. Of those that a mesh axis runs over, the one named last changes fastest.
Arguments:
- conv_input: bfloat16 [12, 4096, 10240], P('pool', 'seq'), may hold values from -6 to 6
- dt_raw: bfloat16 [12, 4096, 128], P('pool', 'seq'), may hold values from -5 to 5
- gate_z: bfloat16 [12, 4096, 8192], P('pool', 'seq'), may hold values from -6 to 6
- conv_weight: float32 [4, 10240], replicated, may hold values from -3 to 3
- dt_bias: float32 [128], P('seq'), may hold values from -2.5 to -0.5
- decay_rate: float32 [128], P('seq'), may hold values from 0.0003 to 0.05
- skip_d: float32 [128], P('seq'), may hold values from 0.5 to 1.5
- norm_gain: float32 [8192], replicated, may hold values from 0.5 to 1.5
- pool_state: bfloat16 [32, 128, 64, 128], P('pool', 'seq'), may hold values from -12 to 12
- pool_tail: bfloat16 [32, 3, 10240], P('pool'), may hold values from -6 to 6
- route_owner: int32 [12], replicated, may hold values from 0 to 3
- route_slot: int32 [12], replicated, may hold values from 0 to 7
- prefix_hit: int32 [12], replicated, may hold values 0 or 1
- lengths: int32 [12], replicated, may hold values from 1024 to 4096, as said below
Outputs:
- mixed_out: bfloat16 [12, 4096, 8192], P('pool', 'seq')
- final_state: float32 [12, 128, 64, 128], P('pool', 'seq')
The draws below stay inside these ranges and needn't reach their ends.
Inputs may be any that keep to these rules, and one draw needn't show every extreme that they name: `lengths`: some sequence has all 4096 positions valid.
All inputs are finite; a program needn't handle non-finite values.
Results may differ from the reference program's by a relative error of at most 0.0051.
Values may be sent and summed in bfloat16 or wider, within the bound.
No kernel may reach another device: no remote copies, remote signals or barrier semaphores. Data moves between devices by JAX's collectives and lax.ppermute only.
A program may use at most 128 MiB of HBM per device.

```python
import math
import jax
import jax.numpy as jnp
from jax import lax

HEADS = 128
HEAD_DIM = 64
STATE = 128
GROUPS = 8
KERNEL = 4
BLOCK = 256
STRETCH = 4096
SLOTS = 8
SEQS = 12
POOL_SLOTS = 32
INNER = 8192
CONV_CH = 10240
N_POOL = 4


def draw_lengths(key, part):
    first, second = jax.random.split(jax.random.fold_in(key, 17))
    drawn = jax.random.randint(first, (SEQS,), STRETCH // 4, STRETCH + 1)
    chosen = jax.random.randint(second, (), 0, SEQS)
    return drawn.at[chosen].set(STRETCH).astype(jnp.int32)


def place_ends(values, own_key, low, largest):
    spot = [jax.random.randint(jax.random.fold_in(own_key, axis), (), 0, length) for axis, length in enumerate(values.shape)]
    widest = values.shape.index(max(values.shape))
    neighbour = spot[:widest] + [(spot[widest] + 1) % values.shape[widest]] + spot[widest + 1:]
    return values.at[tuple(spot)].set(low).at[tuple(neighbour)].set(largest)


def block_scale(rng, dims, cuts, low, top_value):
    factor_of = 1.0
    for position, blocks in cuts:
        draws = jax.random.uniform(jax.random.fold_in(jax.random.fold_in(rng, 6), position), (blocks,), jnp.float32, low / len(cuts), top_value / len(cuts))
        factor_of = factor_of * jnp.repeat(jnp.exp(draws), dims[position] // blocks).reshape((-1,) + (1,) * (len(dims) - 1 - position))
    return factor_of


def scatter_about(key, extent, width, reach, cuts=(), kind=jnp.bfloat16):
    level = block_scale(key, extent, cuts, -0.22, 0.18) if cuts else 1.0
    entries = jax.random.normal(key, extent, jnp.float32) * width * level
    return jnp.minimum(jnp.maximum(entries, -reach), reach).astype(kind)


def setup_inputs(seed: int = 0) -> dict:
    arg_keys = jax.random.split(jax.random.key(seed), 15)
    return {
        "conv_input": scatter_about(arg_keys[0], (SEQS, STRETCH, CONV_CH), 1.0, 6.0, ((0, 4), (1, 64))),
        "dt_raw": scatter_about(arg_keys[1], (SEQS, STRETCH, HEADS), 1.0, 5.0, ((0, 4), (1, 64))),
        "gate_z": scatter_about(arg_keys[2], (SEQS, STRETCH, INNER), 1.0, 6.0, ((0, 4), (1, 64))),
        "conv_weight": scatter_about(arg_keys[3], (KERNEL, CONV_CH), KERNEL ** -0.5, 3.0, (), jnp.float32),
        "dt_bias": jnp.clip(-2.5 + 2.0 * jax.random.uniform(arg_keys[4], (HEADS,), jnp.float32) ** block_scale(arg_keys[4], (HEADS,), ((0, 64),), -0.2, 0.2), -2.5, -0.5),
        "decay_rate": jnp.clip(jnp.exp(math.log(0.05) - 5.115996 * jax.random.uniform(arg_keys[5], (HEADS,), jnp.float32) ** block_scale(arg_keys[5], (HEADS,), ((0, 64),), -0.2, 0.2)), 0.0003, 0.05),
        "skip_d": jnp.clip(0.5 + 1.0 * jax.random.uniform(arg_keys[6], (HEADS,), jnp.float32) ** block_scale(arg_keys[6], (HEADS,), ((0, 64),), -0.2, 0.2), 0.5, 1.5),
        "norm_gain": jnp.clip(1.0 + 0.1 * jax.random.normal(arg_keys[7], (INNER,), jnp.float32), 0.5, 1.5),
        "pool_state": scatter_about(arg_keys[8], (POOL_SLOTS, HEADS, HEAD_DIM, STATE), 2.0, 12.0, ((0, 4), (1, 64))),
        "pool_tail": scatter_about(arg_keys[9], (POOL_SLOTS, KERNEL - 1, CONV_CH), 1.0, 6.0, ((0, 4),)),
        "route_owner": place_ends(jax.random.randint(arg_keys[10], (SEQS,), 0, N_POOL), jax.random.fold_in(arg_keys[10], 1), 0, N_POOL - 1).astype(jnp.int32),
        "route_slot": place_ends(jax.random.randint(arg_keys[11], (SEQS,), 0, SLOTS), jax.random.fold_in(arg_keys[11], 1), 0, SLOTS - 1).astype(jnp.int32),
        "prefix_hit": place_ends((jax.random.randint(arg_keys[12], (SEQS,), 0, 4) < 3).astype(jnp.int32), jax.random.fold_in(arg_keys[12], 1), 0, 1),
        "lengths": draw_lengths(jax.random.fold_in(arg_keys[14], 71), 0),
    }


norm_eps = 1e-05

def conv_apply(padded_in, weight, stretch_len):
    summed = weight[0] * padded_in[..., 0:stretch_len, :]
    for offset in range(1, weight.shape[0]):
        summed = summed + weight[offset] * padded_in[..., offset:offset + stretch_len, :]
    return jax.nn.silu(summed)

def block_scan(x_part, b_part, c_part, step_size, rate, skip, start_state):
    stretch_len = x_part.shape[0]
    block_count = stretch_len // BLOCK
    lower_tri = jnp.arange(BLOCK)[:, None] >= jnp.arange(BLOCK)[None, :]

    def blocked(source):
        return source.reshape((block_count, BLOCK) + source.shape[1:])

    def per_block(carry_state, pieces):
        x_blk, b_blk, c_blk, dt_blk = pieces
        cum_decay = jnp.cumsum(-rate * dt_blk, axis=0)
        cum_heads = jnp.transpose(cum_decay, (1, 2, 0))
        log_gap = cum_heads[..., :, None] - cum_heads[..., None, :]
        decay_mat = jnp.where(lower_tri, jnp.exp(jnp.where(lower_tri, log_gap, 0.0)), 0.0)
        scores = jnp.einsum('tgn,sgn->gts', c_blk.astype(jnp.float32), b_blk.astype(jnp.float32))
        dt_heads = jnp.transpose(dt_blk, (1, 2, 0))
        weights = (scores[:, None] * decay_mat * dt_heads[:, :, None, :]).astype(jnp.bfloat16)
        intra_out = jnp.einsum('gets,sgep->tgep', weights.astype(jnp.float32), x_blk.astype(jnp.float32))
        carried = jnp.exp(cum_decay)[..., None] * jnp.einsum('tgn,gepn->tgep', c_blk.astype(jnp.float32), carry_state, precision=lax.Precision.HIGHEST)
        block_out = intra_out + carried + skip[..., None] * x_blk.astype(jnp.float32)
        tail_weight = jnp.exp(cum_decay[-1][None] - cum_decay) * dt_blk
        scaled = (tail_weight[..., None] * x_blk.astype(jnp.float32)).astype(jnp.bfloat16)
        new_state = jnp.exp(cum_decay[-1])[..., None, None] * carry_state + jnp.einsum('sgep,sgn->gepn', scaled.astype(jnp.float32), b_blk.astype(jnp.float32))
        return (new_state, block_out)
    last_state, block_outs = lax.scan(per_block, start_state, (blocked(x_part), blocked(b_part), blocked(c_part), blocked(step_size)))
    return (block_outs.reshape((stretch_len,) + block_outs.shape[2:]), last_state)

def reference(conv_input, dt_raw, gate_z, conv_weight, dt_bias, decay_rate, skip_d, norm_gain, pool_state, pool_tail, route_owner, route_slot, prefix_hit, lengths):
    inner_width = HEADS * HEAD_DIM
    group_heads = HEADS // GROUPS
    rate = decay_rate.reshape(GROUPS, group_heads)
    skip = skip_d.reshape(GROUPS, group_heads)

    def per_seq(index):
        pool_row = (route_owner[index] * SLOTS + route_slot[index]).astype(jnp.int32)
        hit_scale = prefix_hit[index].astype(jnp.float32)
        seed_state = lax.dynamic_index_in_dim(pool_state, pool_row, 0, keepdims=False).astype(jnp.float32) * hit_scale
        seed_tail = lax.dynamic_index_in_dim(pool_tail, pool_row, 0, keepdims=False).astype(jnp.float32) * hit_scale
        valid = (jnp.arange(STRETCH, dtype=jnp.int32) < lengths[index]).astype(jnp.float32)
        seq_input = lax.dynamic_index_in_dim(conv_input, index, 0, keepdims=False).astype(jnp.float32)
        padded_in = jnp.concatenate([seed_tail, seq_input], axis=0)
        conv_out = (conv_apply(padded_in, conv_weight, STRETCH) * valid[:, None]).astype(jnp.bfloat16)
        x_conv = conv_out[:, :inner_width].reshape(STRETCH, GROUPS, group_heads, HEAD_DIM)
        b_conv = conv_out[:, inner_width:inner_width + GROUPS * STATE].reshape(STRETCH, GROUPS, STATE)
        c_conv = conv_out[:, inner_width + GROUPS * STATE:].reshape(STRETCH, GROUPS, STATE)
        dt_seq = lax.dynamic_index_in_dim(dt_raw, index, 0, keepdims=False).astype(jnp.float32)
        step_size = jax.nn.softplus(dt_seq + dt_bias) * valid[:, None]
        ssd_out, last_state = block_scan(x_conv, b_conv, c_conv, step_size.reshape(STRETCH, GROUPS, group_heads), rate, skip, seed_state.reshape(GROUPS, group_heads, HEAD_DIM, STATE))
        ssd_out = ssd_out.reshape(STRETCH, inner_width).astype(jnp.bfloat16)
        gate_seq = lax.dynamic_index_in_dim(gate_z, index, 0, keepdims=False).astype(jnp.float32)
        gated = (ssd_out.astype(jnp.float32) * jax.nn.silu(gate_seq)).reshape(STRETCH, GROUPS, inner_width // GROUPS)
        normed = gated * lax.rsqrt(lax.optimization_barrier(jnp.mean(gated * gated, axis=-1, keepdims=True)) + norm_eps)
        mixed = normed.reshape(STRETCH, inner_width) * norm_gain * valid[:, None]
        return (mixed.astype(jnp.bfloat16), last_state.reshape(HEADS, HEAD_DIM, STATE))
    mixed_out, final_state = lax.map(per_seq, jnp.arange(SEQS, dtype=jnp.int32))
    return (mixed_out, final_state)
```

```python
import functools

import jax
import jax.numpy as jnp
from jax import lax
from jax.experimental import pallas as pl
from jax.experimental.pallas import tpu as pltpu
from jax.sharding import Mesh, PartitionSpec as P

HEADS = 128
HEAD_DIM = 64
STATE = 128
GROUPS = 8
GROUP_HEADS = HEADS // GROUPS
INNER = HEADS * HEAD_DIM
GROUP_X = GROUP_HEADS * HEAD_DIM
GROUP_CH = GROUP_X + 2 * STATE
ROWS = 64
SLAB = GROUPS * ROWS
EXT = 16

norm_eps = 1e-05
f32 = jnp.float32
bf16 = jnp.bfloat16


def params(vmem=48):
    return pltpu.CompilerParams(vmem_limit_bytes=vmem << 20)


def silu(v):
    half = 0.5 * v
    return half + half * jnp.tanh(half)


def split3(v):
    hi = v.astype(bf16)
    rest = v - hi.astype(f32)
    mid = rest.astype(bf16)
    lo = (rest - mid.astype(f32)).astype(bf16)
    return hi, mid, lo


def lane_pack(v):
    lane = lax.broadcasted_iota(jnp.int32, v.shape, 1)
    hi, mid, lo = (part.astype(f32) for part in split3(v))
    packed = jnp.where(lane < 16, hi, jnp.where(lane < 32, mid, jnp.where(lane < 48, lo, 0.0)))
    return packed.astype(bf16)


def dot(a, b, ca=1, cb=0):
    return lax.dot_general(a, b, (((ca,), (cb,)), ((), ())), preferred_element_type=f32)


def pack_body(x_ref, b_ref, c_ref, out_ref):
    out_ref[0, :, :, 0:GROUP_X] = x_ref[...]
    out_ref[0, :, :, GROUP_X : GROUP_X + STATE] = b_ref[...]
    out_ref[0, :, :, GROUP_X + STATE : GROUP_CH] = c_ref[...]


def pack_groups(conv_input, first, count):
    block = first // count
    b_at = INNER // STATE
    return pl.pallas_call(
        pack_body,
        grid=(GROUPS,),
        in_specs=[
            pl.BlockSpec((count, ROWS, GROUP_X), lambda g: (block, 0, g)),
            pl.BlockSpec((count, ROWS, STATE), lambda g: (block, 0, b_at + g)),
            pl.BlockSpec((count, ROWS, STATE), lambda g: (block, 0, b_at + GROUPS + g)),
        ],
        out_specs=pl.BlockSpec((1, count, ROWS, GROUP_CH), lambda g: (g, 0, 0, 0)),
        out_shape=jax.ShapeDtypeStruct((GROUPS, count, ROWS, GROUP_CH), bf16),
        compiler_params=params(),
        name="pack_groups",
    )(conv_input, conv_input, conv_input)


def steps_body(meta_ref, dt_ref, par_ref, ein_ref, eout_ref, rows_ref):
    s = pl.program_id(0)
    z, j, length = meta_ref[0], meta_ref[1], meta_ref[2 + s]
    par = jnp.sum(par_ref[...], axis=0)
    bias, rate, skip = par[0:1], par[1:2], par[2:3]
    src = lax.broadcasted_iota(jnp.int32, (128, 128), 0)
    dst = lax.broadcasted_iota(jnp.int32, (128, 128), 1)
    sel = ((src == j * GROUP_HEADS + (dst & 15)) & (dst < 48)).astype(f32).astype(bf16)
    raw = dot(dt_ref[...].reshape(SLAB, 128).astype(bf16), sel)
    pos = z * SLAB + lax.broadcasted_iota(jnp.int32, (SLAB, 128), 0)
    arg = raw + bias
    dt = jnp.maximum(arg, 0.0) + jnp.log1p(jnp.exp(-jnp.abs(arg)))
    dt = jnp.where(pos < length, dt, 0.0)
    rise = -rate * dt
    row = lax.broadcasted_iota(jnp.int32, (SLAB, SLAB), 0)
    col = lax.broadcasted_iota(jnp.int32, (SLAB, SLAB), 1)
    tri = (row >= col).astype(f32).astype(bf16)
    hi, mid, lo = split3(rise)
    cum = dot(tri, hi) + dot(tri, mid) + dot(tri, lo)
    middle = 0.5 * cum[SLAB - 1 : SLAB]
    ein_ref[0] = lane_pack(jnp.exp(middle - cum) * dt)
    eout_ref[0] = lane_pack(jnp.exp(cum - middle))
    which = lax.broadcasted_iota(jnp.int32, (EXT, 128), 0)
    rows_ref[0] = lane_pack(jnp.where(which == 0, jnp.exp(middle), skip) + jnp.zeros((EXT, 128), f32))


def step_factors(meta, dt_all, par_all, seqs):
    return pl.pallas_call(
        steps_body,
        grid_spec=pltpu.PrefetchScalarGridSpec(
            num_scalar_prefetch=1,
            grid=(seqs,),
            in_specs=[
                pl.BlockSpec((GROUPS, ROWS, 128), lambda s, m: (0, s, 0)),
                pl.BlockSpec((GROUPS, 8, 128), lambda s, m: (0, 0, 0)),
            ],
            out_specs=[
                pl.BlockSpec((1, SLAB, 128), lambda s, m: (s, 0, 0)),
                pl.BlockSpec((1, SLAB, 128), lambda s, m: (s, 0, 0)),
                pl.BlockSpec((1, EXT, 128), lambda s, m: (s, 0, 0)),
            ],
        ),
        out_shape=[
            jax.ShapeDtypeStruct((seqs, SLAB, 128), bf16),
            jax.ShapeDtypeStruct((seqs, SLAB, 128), bf16),
            jax.ShapeDtypeStruct((seqs, EXT, 128), bf16),
        ],
        compiler_params=params(),
        name="step_factors",
    )(meta, dt_all, par_all)


def conv_body(first, meta_ref, recv_ref, halo_ref, w_ref, ein_ref, rows_ref, e3_ref, xbc_ref, sout_ref, xs):
    s = pl.program_id(0)
    z, length = meta_ref[0], meta_ref[2 + first + s]
    xs[0:8, :] = halo_ref[0]
    for b in range(GROUPS):
        xs[8 + ROWS * b : 8 + ROWS * (b + 1), :] = recv_ref[b, 0].astype(f32)

    def per_rows(b, _):
        start = pl.multiple_of(b * ROWS, ROWS)
        pos = z * SLAB + start + lax.broadcasted_iota(jnp.int32, (ROWS, 256), 0)
        keep = pos < length
        for lane in range(0, GROUP_CH, 256):
            win = xs[pl.ds(start, ROWS + 8), lane : lane + 256]
            acc = w_ref[3:4, lane : lane + 256] * win[8:]
            for back in (1, 2, 3):
                acc = acc + w_ref[3 - back : 4 - back, lane : lane + 256] * pltpu.roll(win, back, 0)[8:]
            xbc_ref[0, pl.ds(start, ROWS), lane : lane + 256] = jnp.where(keep, silu(acc), 0.0).astype(bf16)
        return 0

    lax.fori_loop(0, GROUPS, per_rows, 0)
    e3 = e3_ref[...]
    scaled = (xbc_ref[0, :, 0:GROUP_X].astype(f32) * dot(ein_ref[0], e3)).astype(bf16)
    state = dot(xbc_ref[0, :, GROUP_X : GROUP_X + STATE], scaled, 0, 0)
    grow = dot(rows_ref[0], e3)[0:1]
    state = (state * grow).astype(bf16)
    which = lax.broadcasted_iota(jnp.int32, (EXT, GROUP_X), 0)
    hi, mid, lo = (part.astype(f32) for part in split3(grow))
    extra = jnp.where(which == 0, hi, jnp.where(which == 1, mid, jnp.where(which == 2, lo, 0.0))).astype(bf16)
    for k in range(GROUPS):
        sout_ref[k, 0, 0:STATE, :] = state[:, 128 * k : 128 * (k + 1)]
        sout_ref[k, 0, STATE : STATE + EXT, :] = extra[:, 128 * k : 128 * (k + 1)]


def conv_and_state(meta, recv, halo, weight, ein, rows, e3, first, count):
    return pl.pallas_call(
        functools.partial(conv_body, first),
        grid_spec=pltpu.PrefetchScalarGridSpec(
            num_scalar_prefetch=1,
            grid=(count,),
            in_specs=[
                pl.BlockSpec((GROUPS, 1, ROWS, GROUP_CH), lambda s, m: (0, s, 0, 0)),
                pl.BlockSpec((1, 8, GROUP_CH), lambda s, m: (s, 0, 0)),
                pl.BlockSpec((4, GROUP_CH), lambda s, m: (0, 0)),
                pl.BlockSpec((1, SLAB, 128), lambda s, m: (first + s, 0, 0)),
                pl.BlockSpec((1, EXT, 128), lambda s, m: (first + s, 0, 0)),
                pl.BlockSpec((128, GROUP_X), lambda s, m: (0, 0)),
            ],
            out_specs=[
                pl.BlockSpec((1, SLAB, GROUP_CH), lambda s, m: (s, 0, 0)),
                pl.BlockSpec((GROUPS, 1, STATE + EXT, 128), lambda s, m: (0, s, 0, 0)),
            ],
            scratch_shapes=[pltpu.VMEM((SLAB + 8, GROUP_CH), f32)],
        ),
        out_shape=[
            jax.ShapeDtypeStruct((count, SLAB, GROUP_CH), bf16),
            jax.ShapeDtypeStruct((GROUPS, count, STATE + EXT, 128), bf16),
        ],
        compiler_params=params(),
        name="conv_and_state",
    )(meta, recv, halo, weight, ein, rows, e3)


def inner_body(xbc_ref, ein_ref, eout_ref, rows_ref, e3_ref, out_ref):
    e3 = e3_ref[...]
    x = xbc_ref[0, :, 0:GROUP_X]
    scaled = (x.astype(f32) * dot(ein_ref[0], e3)).astype(bf16)
    skip = dot(rows_ref[0], e3)[1:2]
    half = SLAB // 2
    for part in range(2):
        rows = slice(part * half, (part + 1) * half)
        upto = (part + 1) * half
        c_part = xbc_ref[0, rows, GROUP_X + STATE : GROUP_CH]
        b_part = xbc_ref[0, 0:upto, GROUP_X : GROUP_X + STATE]
        scores = dot(c_part, b_part, 1, 1)
        t_at = part * half + lax.broadcasted_iota(jnp.int32, (half, upto), 0)
        u_at = lax.broadcasted_iota(jnp.int32, (half, upto), 1)
        scores = jnp.where(u_at <= t_at, scores, 0.0).astype(bf16)
        acc = dot(scores, scaled[0:upto])
        out_ref[0, rows, :] = dot(eout_ref[0, rows, :], e3) * acc + skip * x[rows].astype(f32)


def inner_output(xbc, ein, eout, rows, e3, first, count):
    return pl.pallas_call(
        inner_body,
        grid=(count,),
        in_specs=[
            pl.BlockSpec((1, SLAB, GROUP_CH), lambda s: (s, 0, 0)),
            pl.BlockSpec((1, SLAB, 128), lambda s: (first + s, 0, 0)),
            pl.BlockSpec((1, SLAB, 128), lambda s: (first + s, 0, 0)),
            pl.BlockSpec((1, EXT, 128), lambda s: (first + s, 0, 0)),
            pl.BlockSpec((128, GROUP_X), lambda s: (0, 0)),
        ],
        out_specs=pl.BlockSpec((1, SLAB, GROUP_X), lambda s: (s, 0, 0)),
        out_shape=jax.ShapeDtypeStruct((count, SLAB, GROUP_X), f32),
        compiler_params=params(),
        name="inner_output",
    )(xbc, ein, eout, rows, e3)


def scan_body(got_ref, seed_ref, start_ref, final_ref):
    state = seed_ref[0].astype(f32).T
    for k in range(got_ref.shape[0]):
        start_ref[k, 0] = state.astype(bf16)
        extra = got_ref[k, 0, STATE : STATE + EXT, :].astype(f32)
        root = extra[0:1] + extra[1:2] + extra[2:3]
        state = (root * root) * state + got_ref[k, 0, 0:STATE, :].astype(f32)
    final_ref[0] = state.T


def scan_slabs(got, seed, first, count):
    slabs = got.shape[0]
    return pl.pallas_call(
        scan_body,
        grid=(count,),
        in_specs=[
            pl.BlockSpec((slabs, 1, STATE + EXT, 128), lambda s: (0, s, 0, 0)),
            pl.BlockSpec((1, 128, STATE), lambda s: (first + s, 0, 0)),
        ],
        out_specs=[
            pl.BlockSpec((slabs, 1, STATE, 128), lambda s: (0, s, 0, 0)),
            pl.BlockSpec((1, 128, STATE), lambda s: (s, 0, 0)),
        ],
        out_shape=[
            jax.ShapeDtypeStruct((slabs, count, STATE, 128), bf16),
            jax.ShapeDtypeStruct((count, 128, STATE), f32),
        ],
        compiler_params=params(),
        name="scan_slabs",
    )(got, seed)


def finish_body(part_ref, c_ref, start_ref, eout_ref, rows_ref, e3_ref, out_ref):
    e3 = e3_ref[...]
    grow = dot(rows_ref[0], e3)[0:1]
    state = jnp.concatenate([start_ref[k, 0] for k in range(GROUPS)], axis=1)
    carried = dot(c_ref[0], state)
    total = part_ref[0] + dot(eout_ref[0], e3) * grow * carried
    for b in range(GROUPS):
        out_ref[b, 0] = total[ROWS * b : ROWS * (b + 1)].astype(bf16)


def finish_output(part, xbc, start, eout, rows, e3, first, count):
    c_at = GROUP_CH // STATE - 1
    return pl.pallas_call(
        finish_body,
        grid=(count,),
        in_specs=[
            pl.BlockSpec((1, SLAB, GROUP_X), lambda s: (s, 0, 0)),
            pl.BlockSpec((1, SLAB, STATE), lambda s: (s, 0, c_at)),
            pl.BlockSpec((GROUPS, 1, STATE, 128), lambda s: (0, s, 0, 0)),
            pl.BlockSpec((1, SLAB, 128), lambda s: (first + s, 0, 0)),
            pl.BlockSpec((1, EXT, 128), lambda s: (first + s, 0, 0)),
            pl.BlockSpec((128, GROUP_X), lambda s: (0, 0)),
        ],
        out_specs=pl.BlockSpec((GROUPS, 1, ROWS, GROUP_X), lambda s: (0, s, 0, 0)),
        out_shape=jax.ShapeDtypeStruct((GROUPS, count, ROWS, GROUP_X), bf16),
        compiler_params=params(),
        name="finish_output",
    )(part, xbc, start, eout, rows, e3)


def norm_body(meta_ref, y_ref, gate_ref, gain_ref, out_ref):
    at = (meta_ref[0] * GROUPS + meta_ref[1]) * ROWS
    gain = gain_ref[...]
    for s in range(out_ref.shape[0]):
        gated = y_ref[0, s].astype(f32) * silu(gate_ref[s].astype(f32))
        mean = jnp.mean(gated * gated, axis=-1, keepdims=True)
        pos = at + lax.broadcasted_iota(jnp.int32, (ROWS, 1), 0)
        scale = jnp.where(pos < meta_ref[2 + s], lax.rsqrt(mean + norm_eps), 0.0)
        out_ref[s] = (gated * scale * gain).astype(bf16)


def gated_norm(meta, y, gate_z, gain, seqs):
    return pl.pallas_call(
        norm_body,
        grid_spec=pltpu.PrefetchScalarGridSpec(
            num_scalar_prefetch=1,
            grid=(GROUPS,),
            in_specs=[
                pl.BlockSpec((1, seqs, ROWS, GROUP_X), lambda g, m: (g, 0, 0, 0)),
                pl.BlockSpec((seqs, ROWS, GROUP_X), lambda g, m: (0, 0, g)),
                pl.BlockSpec((1, GROUP_X), lambda g, m: (0, g)),
            ],
            out_specs=pl.BlockSpec((seqs, ROWS, GROUP_X), lambda g, m: (0, 0, g)),
        ),
        out_shape=jax.ShapeDtypeStruct((seqs, ROWS, INNER), bf16),
        compiler_params=params(),
        name="gated_norm",
    )(meta, y, gate_z, gain)


def local(
    conv_input,
    dt_raw,
    gate_z,
    conv_weight,
    dt_bias,
    decay_rate,
    skip_d,
    norm_gain,
    pool_state,
    pool_tail,
    route_owner,
    route_slot,
    prefix_hit,
    lengths,
):
    seqs = conv_input.shape[0]
    slabs = lax.axis_size("z")
    z = lax.axis_index("z")
    j = lax.axis_index("j")
    first_seq = lax.axis_index("pool") * seqs
    slot_count = pool_state.shape[0]
    flip = [(a * GROUPS + b, b * GROUPS + a) for a in range(slabs) for b in range(GROUPS)]

    def group_columns(source):
        last = source.ndim - 1
        return jnp.concatenate(
            [
                lax.dynamic_slice_in_dim(source, j * GROUP_X, GROUP_X, last),
                lax.dynamic_slice_in_dim(source, INNER + j * STATE, STATE, last),
                lax.dynamic_slice_in_dim(source, INNER + (GROUPS + j) * STATE, STATE, last),
            ],
            axis=-1,
        )

    sent = pack_groups(conv_input, 0, seqs)
    recv = lax.all_to_all(sent, "j", 0, 0, tiled=True)

    valid_len = lax.dynamic_slice_in_dim(lengths, first_seq, seqs)
    hit = lax.dynamic_slice_in_dim(prefix_hit, first_seq, seqs)
    owner = lax.dynamic_slice_in_dim(route_owner, first_seq, seqs)
    slot = lax.dynamic_slice_in_dim(route_slot, first_seq, seqs)
    pick = owner * slot_count + slot
    meta = jnp.concatenate([jnp.stack([z, j]).astype(jnp.int32), valid_len])

    whole_state = lax.all_gather(pool_state, "pool", axis=0, tiled=True)
    seed = jnp.take(whole_state, pick, axis=0) * hit.astype(bf16)[:, None, None, None]
    seed = lax.ppermute(seed.reshape(seqs, 128, STATE), ("z", "j"), flip)

    whole_tail = lax.all_gather(group_columns(pool_tail), "pool", axis=0, tiled=True)
    tail = jnp.take(whole_tail, pick, axis=0) * hit.astype(bf16)[:, None, None]

    lane = jnp.arange(128, dtype=jnp.int32)
    own = jnp.stack([dt_bias, decay_rate, skip_d])
    here = (lane < 48) & ((lane & 15) // 2 == j)
    par = jnp.where(here, jnp.where(lane & 1 == 0, own[:, 0:1], own[:, 1:2]), 0.0)
    par = jnp.pad(par, ((0, 5), (0, 0)))
    mine = jnp.concatenate([dt_raw.reshape(seqs * ROWS, 128).astype(f32), par], axis=0)
    both = lax.all_gather(mine, "j", axis=0, tiled=False)
    par_all = lax.ppermute(both[:, seqs * ROWS :], ("z", "j"), flip)
    ein, eout, rows = step_factors(meta, both, par_all, seqs)

    head_of = jnp.arange(GROUP_X, dtype=jnp.int32)[None, :] // HEAD_DIM
    src = jnp.arange(128, dtype=jnp.int32)[:, None]
    e3 = ((src < 48) & ((src & 15) == head_of)).astype(bf16)
    weight = group_columns(conv_weight)

    before = lax.ppermute(recv[GROUPS - 1, :, ROWS - 3 :], "z", [(k, k + 1) for k in range(slabs - 1)])
    halo = jnp.where(z == 0, tail, before).astype(f32)
    halo = jnp.pad(halo, ((0, 0), (5, 0), (0, 0)))

    xbc, sout = conv_and_state(meta, recv, halo, weight, ein, rows, e3, 0, seqs)
    got = lax.all_to_all(sout, "z", 0, 0, tiled=True)
    part = inner_output(xbc, ein, eout, rows, e3, 0, seqs)
    start, final = scan_slabs(got, seed, 0, seqs)
    back = lax.all_to_all(start, "z", 0, 0, tiled=True)
    final = lax.ppermute(final, ("z", "j"), flip)
    y = finish_output(part, xbc, back, eout, rows, e3, 0, seqs)
    token = lax.all_to_all(y, "j", 0, 0, tiled=True)
    mixed = gated_norm(meta, token, gate_z, norm_gain.reshape(1, INNER), seqs)
    return (mixed, final.reshape(seqs, 2, HEAD_DIM, STATE))


def solution(mesh):
    seq_count, pool_count = mesh.devices.shape
    split = Mesh(mesh.devices.reshape(seq_count // GROUPS, GROUPS, pool_count), ("z", "j", "pool"))
    seq = ("z", "j")
    in_specs = (
        P("pool", seq, None),
        P("pool", seq, None),
        P("pool", seq, None),
        P(),
        P(seq),
        P(seq),
        P(seq),
        P(),
        P("pool", seq, None, None),
        P("pool", None, None),
        P(),
        P(),
        P(),
        P(),
    )
    out_specs = (P("pool", seq, None), P("pool", seq, None, None))
    return jax.shard_map(local, mesh=split, in_specs=in_specs, out_specs=out_specs, check_vma=False)
```

```python
import functools

import jax
import jax.numpy as jnp
from jax import lax
from jax.experimental import pallas as pl
from jax.experimental.pallas import tpu as pltpu
from jax.sharding import Mesh, PartitionSpec as P

HEADS = 128
HEAD_DIM = 64
STATE = 128
GROUPS = 8
GROUP_HEADS = HEADS // GROUPS
INNER = HEADS * HEAD_DIM
GROUP_X = GROUP_HEADS * HEAD_DIM
GROUP_CH = GROUP_X + 2 * STATE
ROWS = 64
SLAB = GROUPS * ROWS
EXT = 16

norm_eps = 1e-05
f32 = jnp.float32
bf16 = jnp.bfloat16


def params(vmem=24):
    return pltpu.CompilerParams(vmem_limit_bytes=vmem << 20)


def silu(v):
    half = 0.5 * v
    return half + half * jnp.tanh(half)


def split3(v):
    hi = v.astype(bf16)
    rest = v - hi.astype(f32)
    mid = rest.astype(bf16)
    lo = (rest - mid.astype(f32)).astype(bf16)
    return hi, mid, lo


def lane_pack(v):
    lane = lax.broadcasted_iota(jnp.int32, v.shape, 1)
    hi, mid, lo = (part.astype(f32) for part in split3(v))
    packed = jnp.where(lane < 16, hi, jnp.where(lane < 32, mid, jnp.where(lane < 48, lo, 0.0)))
    return packed.astype(bf16)


def dot(a, b, ca=1, cb=0):
    return lax.dot_general(a, b, (((ca,), (cb,)), ((), ())), preferred_element_type=f32)


def in_hbm(v):
    return pltpu.with_memory_space_constraint(v, pltpu.HBM)


def pack_body(first, x_ref, out_ref, held, in_sems, out_sems):
    count = held.shape[0]
    loads = [pltpu.make_async_copy(x_ref.at[first + s], held.at[s], in_sems.at[s]) for s in range(count)]
    for load in loads:
        load.start()
    stores = []
    for s in range(count):
        loads[s].wait()
        for g in range(GROUPS):
            pieces = (
                (g * GROUP_X, 0, GROUP_X),
                (INNER + g * STATE, GROUP_X, STATE),
                (INNER + (GROUPS + g) * STATE, GROUP_X + STATE, STATE),
            )
            for i, (src, dst, width) in enumerate(pieces):
                store = pltpu.make_async_copy(
                    held.at[s, :, pl.ds(src, width)],
                    out_ref.at[g, s, :, pl.ds(dst, width)],
                    out_sems.at[s, g, i],
                )
                store.start()
                stores.append(store)
    for store in stores:
        store.wait()


def pack_groups(conv_input, first, count):
    return pl.pallas_call(
        functools.partial(pack_body, first),
        in_specs=[pl.BlockSpec(memory_space=pl.ANY)],
        out_specs=pl.BlockSpec(memory_space=pl.ANY),
        out_shape=pltpu.HBM((GROUPS, count, ROWS, GROUP_CH), bf16),
        scratch_shapes=[
            pltpu.VMEM((count,) + conv_input.shape[1:], bf16),
            pltpu.SemaphoreType.DMA((count,)),
            pltpu.SemaphoreType.DMA((count, GROUPS, 3)),
        ],
        compiler_params=params(12),
        name="pack_groups",
    )(in_hbm(conv_input))


def front_body(j_ref, bias_ref, rate_ref, skip_ref, dt_ref, out_ref):
    row = lax.broadcasted_iota(jnp.int32, (EXT, 128), 0)
    lane = lax.broadcasted_iota(jnp.int32, (EXT, 128), 1)
    even = (lane & 1) == 0
    values = jnp.where(even, skip_ref[0], skip_ref[1])
    values = jnp.where(row == 0, jnp.where(even, bias_ref[0], bias_ref[1]), values)
    values = jnp.where(row == 1, jnp.where(even, rate_ref[0], rate_ref[1]), values)
    here = ((lane & 15) >> 1 == j_ref[0]) & (row < 3)
    packed = lane_pack(jnp.where(here, values, 0.0))
    rows = dt_ref.shape[0]
    for g in range(GROUPS):
        out_ref[g, 0:rows, :] = dt_ref[...]
        out_ref[g, rows : rows + EXT, :] = packed


def front_rows(j, dt_bias, decay_rate, skip_d, dt_rows):
    scalar = pl.BlockSpec(memory_space=pltpu.SMEM)
    return pl.pallas_call(
        front_body,
        in_specs=[scalar, scalar, scalar, scalar, pl.BlockSpec(memory_space=pltpu.VMEM)],
        out_specs=pl.BlockSpec(memory_space=pltpu.VMEM),
        out_shape=pltpu.HBM((GROUPS, dt_rows.shape[0] + EXT, 128), bf16),
        compiler_params=params(8),
        name="front_rows",
    )(j.reshape(1), in_hbm(dt_bias), in_hbm(decay_rate), in_hbm(skip_d), in_hbm(dt_rows))


def steps_body(meta_ref, dt_ref, par_ref, ein_ref, eout_ref, rows_ref):
    s = pl.program_id(0)
    z, j, length = meta_ref[0], meta_ref[1], meta_ref[2 + s]
    src = lax.broadcasted_iota(jnp.int32, (128, 128), 0)
    dst = lax.broadcasted_iota(jnp.int32, (128, 128), 1)
    join = ((src & 15) == (dst & 15)) & (src < 48) & (dst < 48)
    par = jnp.sum(par_ref[...].astype(f32), axis=0).astype(bf16)
    par = dot(par, join.astype(f32).astype(bf16))
    bias, rate, skip = par[0:1], par[1:2], par[2:3]
    sel = ((src == j * GROUP_HEADS + (dst & 15)) & (dst < 48)).astype(f32).astype(bf16)
    raw = dot(dt_ref[...].reshape(SLAB, 128), sel)
    pos = z * SLAB + lax.broadcasted_iota(jnp.int32, (SLAB, 128), 0)
    arg = raw + bias
    dt = jnp.maximum(arg, 0.0) + jnp.log1p(jnp.exp(-jnp.abs(arg)))
    dt = jnp.where(pos < length, dt, 0.0)
    rise = -rate * dt
    row = lax.broadcasted_iota(jnp.int32, (SLAB, SLAB), 0)
    col = lax.broadcasted_iota(jnp.int32, (SLAB, SLAB), 1)
    tri = (row >= col).astype(f32).astype(bf16)
    hi, mid, lo = split3(rise)
    cum = dot(tri, hi) + dot(tri, mid) + dot(tri, lo)
    middle = 0.5 * cum[SLAB - 1 : SLAB]
    ein_ref[0] = lane_pack(jnp.exp(middle - cum) * dt)
    eout_ref[0] = lane_pack(jnp.exp(cum - middle))
    which = lax.broadcasted_iota(jnp.int32, (EXT, 128), 0)
    rows_ref[0] = lane_pack(jnp.where(which == 0, jnp.exp(middle), skip) + jnp.zeros((EXT, 128), f32))


def step_factors(meta, dt_all, par_all, seqs):
    return pl.pallas_call(
        steps_body,
        grid_spec=pltpu.PrefetchScalarGridSpec(
            num_scalar_prefetch=1,
            grid=(seqs,),
            in_specs=[
                pl.BlockSpec((GROUPS, ROWS, 128), lambda s, m: (0, s, 0)),
                pl.BlockSpec((GROUPS, EXT, 128), lambda s, m: (0, 0, 0)),
            ],
            out_specs=[
                pl.BlockSpec((1, SLAB, 128), lambda s, m: (s, 0, 0)),
                pl.BlockSpec((1, SLAB, 128), lambda s, m: (s, 0, 0)),
                pl.BlockSpec((1, EXT, 128), lambda s, m: (s, 0, 0)),
            ],
        ),
        out_shape=[
            jax.ShapeDtypeStruct((seqs, SLAB, 128), bf16),
            jax.ShapeDtypeStruct((seqs, SLAB, 128), bf16),
            jax.ShapeDtypeStruct((seqs, EXT, 128), bf16),
        ],
        compiler_params=params(16),
        name="step_factors",
    )(meta, dt_all, par_all)


def conv_body(first, meta_ref, recv_ref, halo_ref, w_ref, ein_ref, rows_ref, e3_ref, xbc_ref, sout_ref, xs, scaled):
    s = pl.program_id(0)
    z, length = meta_ref[0], meta_ref[2 + first + s]
    xs[0:8, :] = halo_ref[0]
    for b in range(GROUPS):
        xs[8 + ROWS * b : 8 + ROWS * (b + 1), :] = recv_ref[b, 0].astype(f32)

    def per_rows(b, _):
        start = pl.multiple_of(b * ROWS, ROWS)
        pos = z * SLAB + start + lax.broadcasted_iota(jnp.int32, (ROWS, 256), 0)
        keep = pos < length
        for lane in range(0, GROUP_CH, 256):
            win = xs[pl.ds(start, ROWS + 8), lane : lane + 256]
            acc = w_ref[3:4, lane : lane + 256] * win[8:]
            for back in (1, 2, 3):
                acc = acc + w_ref[3 - back : 4 - back, lane : lane + 256] * pltpu.roll(win, back, 0)[8:]
            xbc_ref[0, pl.ds(start, ROWS), lane : lane + 256] = jnp.where(keep, acc + acc * jnp.tanh(acc), 0.0).astype(bf16)
        return 0

    lax.fori_loop(0, GROUPS, per_rows, 0)
    e3 = e3_ref[...]
    for b in range(0, SLAB, 128):
        here = slice(b, b + 128)
        scaled[here] = (xbc_ref[0, here, 0:GROUP_X].astype(f32) * dot(ein_ref[0, here], e3)).astype(bf16)
    state = dot(xbc_ref[0, :, GROUP_X : GROUP_X + STATE], scaled[...], 0, 0)
    grow = dot(rows_ref[0], e3)[0:1]
    state = (state * grow).astype(bf16)
    which = lax.broadcasted_iota(jnp.int32, (EXT, GROUP_X), 0)
    hi, mid, lo = (part.astype(f32) for part in split3(grow))
    extra = jnp.where(which == 0, hi, jnp.where(which == 1, mid, jnp.where(which == 2, lo, 0.0))).astype(bf16)
    for k in range(GROUPS):
        sout_ref[k, 0, 0:STATE, :] = state[:, 128 * k : 128 * (k + 1)]
        sout_ref[k, 0, STATE : STATE + EXT, :] = extra[:, 128 * k : 128 * (k + 1)]


def conv_and_state(meta, recv, halo, weight, ein, rows, e3, first, count):
    return pl.pallas_call(
        functools.partial(conv_body, first),
        grid_spec=pltpu.PrefetchScalarGridSpec(
            num_scalar_prefetch=1,
            grid=(count,),
            in_specs=[
                pl.BlockSpec((GROUPS, 1, ROWS, GROUP_CH), lambda s, m: (0, s, 0, 0)),
                pl.BlockSpec((1, 8, GROUP_CH), lambda s, m: (s, 0, 0)),
                pl.BlockSpec((4, GROUP_CH), lambda s, m: (0, 0)),
                pl.BlockSpec((1, SLAB, 128), lambda s, m: (first + s, 0, 0)),
                pl.BlockSpec((1, EXT, 128), lambda s, m: (first + s, 0, 0)),
                pl.BlockSpec((128, GROUP_X), lambda s, m: (0, 0)),
            ],
            out_specs=[
                pl.BlockSpec((1, SLAB, GROUP_CH), lambda s, m: (s, 0, 0)),
                pl.BlockSpec((GROUPS, 1, STATE + EXT, 128), lambda s, m: (0, s, 0, 0)),
            ],
            scratch_shapes=[pltpu.VMEM((SLAB + 8, GROUP_CH), f32), pltpu.VMEM((SLAB, GROUP_X), bf16)],
        ),
        out_shape=[
            pltpu.HBM((count, SLAB, GROUP_CH), bf16),
            pltpu.HBM((GROUPS, count, STATE + EXT, 128), bf16),
        ],
        compiler_params=params(24),
        name="conv_and_state",
    )(meta, in_hbm(recv), halo, weight, ein, rows, e3)


def inner_body(xbc_ref, ein_ref, eout_ref, rows_ref, e3_ref, out_ref):
    e3 = e3_ref[...]
    x = xbc_ref[0, :, 0:GROUP_X]
    scaled = (x.astype(f32) * dot(ein_ref[0], e3)).astype(bf16)
    skip = dot(rows_ref[0], e3)[1:2]
    half = SLAB // 2
    for part in range(2):
        rows = slice(part * half, (part + 1) * half)
        upto = (part + 1) * half
        c_part = xbc_ref[0, rows, GROUP_X + STATE : GROUP_CH]
        b_part = xbc_ref[0, 0:upto, GROUP_X : GROUP_X + STATE]
        scores = dot(c_part, b_part, 1, 1)
        t_at = part * half + lax.broadcasted_iota(jnp.int32, (half, upto), 0)
        u_at = lax.broadcasted_iota(jnp.int32, (half, upto), 1)
        scores = jnp.where(u_at <= t_at, scores, 0.0).astype(bf16)
        acc = dot(scores, scaled[0:upto])
        out_ref[0, rows, :] = dot(eout_ref[0, rows, :], e3) * acc + skip * x[rows].astype(f32)


def inner_output(xbc, ein, eout, rows, e3, first, count):
    return pl.pallas_call(
        inner_body,
        grid=(count,),
        in_specs=[
            pl.BlockSpec((1, SLAB, GROUP_CH), lambda s: (s, 0, 0)),
            pl.BlockSpec((1, SLAB, 128), lambda s: (first + s, 0, 0)),
            pl.BlockSpec((1, SLAB, 128), lambda s: (first + s, 0, 0)),
            pl.BlockSpec((1, EXT, 128), lambda s: (first + s, 0, 0)),
            pl.BlockSpec((128, GROUP_X), lambda s: (0, 0)),
        ],
        out_specs=pl.BlockSpec((1, SLAB, GROUP_X), lambda s: (s, 0, 0)),
        out_shape=pltpu.HBM((count, SLAB, GROUP_X), f32),
        compiler_params=params(24),
        name="inner_output",
    )(in_hbm(xbc), ein, eout, rows, e3)


def scan_body(got_ref, seed_ref, start_ref, final_ref):
    state = seed_ref[0].astype(f32).T
    for k in range(got_ref.shape[0]):
        start_ref[k, 0] = state.astype(bf16)
        extra = got_ref[k, 0, STATE : STATE + EXT, :].astype(f32)
        root = extra[0:1] + extra[1:2] + extra[2:3]
        state = (root * root) * state + got_ref[k, 0, 0:STATE, :].astype(f32)
    final_ref[0] = state.T.astype(bf16)


def scan_slabs(got, seed, first, count):
    slabs = got.shape[0]
    return pl.pallas_call(
        scan_body,
        grid=(count,),
        in_specs=[
            pl.BlockSpec((slabs, 1, STATE + EXT, 128), lambda s: (0, s, 0, 0)),
            pl.BlockSpec((1, 128, STATE), lambda s: (first + s, 0, 0)),
        ],
        out_specs=[
            pl.BlockSpec((slabs, 1, STATE, 128), lambda s: (0, s, 0, 0)),
            pl.BlockSpec((1, 128, STATE), lambda s: (s, 0, 0)),
        ],
        out_shape=[
            pltpu.HBM((slabs, count, STATE, 128), bf16),
            jax.ShapeDtypeStruct((count, 128, STATE), bf16),
        ],
        compiler_params=params(12),
        name="scan_slabs",
    )(got, seed)


def finish_body(part_ref, c_ref, start_ref, eout_ref, rows_ref, e3_ref, out_ref):
    e3 = e3_ref[...]
    grow = dot(rows_ref[0], e3)[0:1]
    state = jnp.concatenate([start_ref[k, 0] for k in range(GROUPS)], axis=1)
    for b in range(out_ref.shape[0]):
        here = slice(ROWS * b, ROWS * (b + 1))
        carried = dot(c_ref[0, here], state)
        out_ref[b, 0] = (part_ref[0, here] + dot(eout_ref[0, here], e3) * (grow * carried)).astype(bf16)


def finish_output(part, xbc, start, eout, rows, e3, first, count):
    c_at = GROUP_CH // STATE - 1
    half = SLAB // 2
    return pl.pallas_call(
        finish_body,
        grid=(count, 2),
        in_specs=[
            pl.BlockSpec((1, half, GROUP_X), lambda s, h: (s, h, 0)),
            pl.BlockSpec((1, half, STATE), lambda s, h: (s, h, c_at)),
            pl.BlockSpec((GROUPS, 1, STATE, 128), lambda s, h: (0, s, 0, 0)),
            pl.BlockSpec((1, half, 128), lambda s, h: (first + s, h, 0)),
            pl.BlockSpec((1, EXT, 128), lambda s, h: (first + s, 0, 0)),
            pl.BlockSpec((128, GROUP_X), lambda s, h: (0, 0)),
        ],
        out_specs=pl.BlockSpec((GROUPS // 2, 1, ROWS, GROUP_X), lambda s, h: (h, s, 0, 0)),
        out_shape=pltpu.HBM((GROUPS, count, ROWS, GROUP_X), bf16),
        compiler_params=params(24),
        name="finish_output",
    )(in_hbm(part), in_hbm(xbc), start, eout, rows, e3)


PAIR = 2


def norm_body(meta_ref, y_ref, gate_ref, gain_ref, out_ref):
    at = (meta_ref[0] * GROUPS + meta_ref[1]) * ROWS
    step = 32
    for q in range(PAIR):
        lanes = slice(GROUP_X * q, GROUP_X * (q + 1))
        gain = gain_ref[:, lanes]
        for s in range(out_ref.shape[0]):
            for row in range(0, ROWS, step):
                here = slice(row, row + step)
                gated = y_ref[q, s, here].astype(f32) * silu(gate_ref[s, here, lanes].astype(f32))
                mean = jnp.mean(gated * gated, axis=-1, keepdims=True)
                pos = at + row + lax.broadcasted_iota(jnp.int32, (step, 1), 0)
                scale = jnp.where(pos < meta_ref[2 + s], lax.rsqrt(mean + norm_eps), 0.0)
                out_ref[s, here, lanes] = (gated * scale * gain).astype(bf16)


def gated_norm(meta, y, gate_z, gain, seqs):
    width = PAIR * GROUP_X
    return pl.pallas_call(
        norm_body,
        grid_spec=pltpu.PrefetchScalarGridSpec(
            num_scalar_prefetch=1,
            grid=(GROUPS // PAIR,),
            in_specs=[
                pl.BlockSpec((PAIR, seqs, ROWS, GROUP_X), lambda g, m: (g, 0, 0, 0)),
                pl.BlockSpec((seqs, ROWS, width), lambda g, m: (0, 0, g)),
                pl.BlockSpec((1, width), lambda g, m: (0, g)),
            ],
            out_specs=pl.BlockSpec((seqs, ROWS, width), lambda g, m: (0, 0, g)),
        ),
        out_shape=pltpu.HBM((seqs, ROWS, INNER), bf16),
        compiler_params=params(20),
        name="gated_norm",
    )(meta, in_hbm(y), gate_z, gain)


def local(
    conv_input,
    dt_raw,
    gate_z,
    conv_weight,
    dt_bias,
    decay_rate,
    skip_d,
    norm_gain,
    pool_state,
    pool_tail,
    route_owner,
    route_slot,
    prefix_hit,
    lengths,
):
    seqs = conv_input.shape[0]
    slabs = lax.axis_size("z")
    z = lax.axis_index("z")
    j = lax.axis_index("j")
    first_seq = lax.axis_index("pool") * seqs
    slot_count = pool_state.shape[0]
    flip = [(a * GROUPS + b, b * GROUPS + a) for a in range(slabs) for b in range(GROUPS)]

    def group_columns(source):
        last = source.ndim - 1
        return jnp.concatenate(
            [
                lax.dynamic_slice_in_dim(source, j * GROUP_X, GROUP_X, last),
                lax.dynamic_slice_in_dim(source, INNER + j * STATE, STATE, last),
                lax.dynamic_slice_in_dim(source, INNER + (GROUPS + j) * STATE, STATE, last),
            ],
            axis=-1,
        )

    front = front_rows(j, dt_bias, decay_rate, skip_d, dt_raw.reshape(seqs * ROWS, 128))
    front = lax.all_to_all(front, "j", 0, 0, tiled=True)
    sent = pack_groups(conv_input, 0, seqs)
    sent, front = lax.optimization_barrier((sent, front))
    recv = lax.all_to_all(sent, "j", 0, 0, tiled=True)

    valid_len = lax.dynamic_slice_in_dim(lengths, first_seq, seqs)
    hit = lax.dynamic_slice_in_dim(prefix_hit, first_seq, seqs)
    owner = lax.dynamic_slice_in_dim(route_owner, first_seq, seqs)
    slot = lax.dynamic_slice_in_dim(route_slot, first_seq, seqs)
    meta = jnp.concatenate([jnp.stack([z, j]).astype(jnp.int32), valid_len])

    pools = lax.axis_size("pool")

    def from_pools(mine):
        parts = [mine]
        for k in range(1, pools):
            parts.append(lax.ppermute(mine, "pool", [(i, (i + k) % pools) for i in range(pools)]))
        return jnp.concatenate(parts, axis=0)

    par_all = lax.ppermute(front[:, seqs * ROWS :], ("z", "j"), flip)
    mine, par_all = lax.optimization_barrier((pool_state.reshape(slot_count, 128, STATE), par_all))
    pick = (lax.axis_index("pool") - owner) % pools * slot_count + slot
    seed = jnp.take(from_pools(mine), pick, axis=0) * hit.astype(bf16)[:, None, None]
    ein, eout, rows = step_factors(meta, front, par_all, seqs)
    tails, seed, ein = lax.optimization_barrier((group_columns(pool_tail), seed, ein))
    seed = lax.ppermute(seed, ("z", "j"), flip)
    tail = jnp.take(from_pools(tails), pick, axis=0) * hit.astype(bf16)[:, None, None]

    head_of = jnp.arange(GROUP_X, dtype=jnp.int32)[None, :] // HEAD_DIM
    src = jnp.arange(128, dtype=jnp.int32)[:, None]
    e3 = ((src < 48) & ((src & 15) == head_of)).astype(bf16)
    weight = 0.5 * group_columns(conv_weight)

    before = lax.ppermute(recv[GROUPS - 1, :, ROWS - 3 :], "z", [(k, k + 1) for k in range(slabs - 1)])
    halo = jnp.where(z == 0, tail, before).astype(f32)
    halo = jnp.pad(halo, ((0, 0), (5, 0), (0, 0)))

    xbc, sout = conv_and_state(meta, recv, halo, weight, ein, rows, e3, 0, seqs)
    sout, seed = lax.optimization_barrier((sout, seed))
    got = lax.all_to_all(sout, "z", 0, 0, tiled=True)
    part = inner_output(xbc, ein, eout, rows, e3, 0, seqs)
    start, final = scan_slabs(got, seed, 0, seqs)
    back = lax.all_to_all(start, "z", 0, 0, tiled=True)
    final = lax.ppermute(final, ("z", "j"), flip)
    y = finish_output(part, xbc, back, eout, rows, e3, 0, seqs)
    token = lax.all_to_all(y, "j", 0, 0, tiled=True)
    mixed = gated_norm(meta, token, gate_z, norm_gain.reshape(1, INNER), seqs)
    return (mixed, final.astype(f32).reshape(seqs, 2, HEAD_DIM, STATE))


def solution(mesh):
    seq_count, pool_count = mesh.devices.shape
    split = Mesh(mesh.devices.reshape(seq_count // GROUPS, GROUPS, pool_count), ("z", "j", "pool"))
    seq = ("z", "j")
    in_specs = (
        P("pool", seq, None),
        P("pool", seq, None),
        P("pool", seq, None),
        P(),
        P(seq),
        P(seq),
        P(seq),
        P(),
        P("pool", seq, None, None),
        P("pool", None, None),
        P(),
        P(),
        P(),
        P(),
    )
    out_specs = (P("pool", seq, None), P("pool", seq, None, None))
    return jax.shard_map(local, mesh=split, in_specs=in_specs, out_specs=out_specs, check_vma=False)
```

```python
import functools

import jax
import jax.numpy as jnp
from jax import lax
from jax.experimental import pallas as pl
from jax.experimental.pallas import tpu as pltpu
from jax.sharding import Mesh, PartitionSpec as P

HEADS = 128
HEAD_DIM = 64
STATE = 128
GROUPS = 8
GROUP_HEADS = HEADS // GROUPS
INNER = HEADS * HEAD_DIM
GROUP_X = GROUP_HEADS * HEAD_DIM
GROUP_CH = GROUP_X + 2 * STATE
ROWS = 64
SLAB = GROUPS * ROWS
EXT = 16

norm_eps = 1e-05
f32 = jnp.float32
bf16 = jnp.bfloat16


def params(vmem=24):
    return pltpu.CompilerParams(vmem_limit_bytes=vmem << 20)


def silu(v):
    half = 0.5 * v
    return half + half * jnp.tanh(half)


def split3(v):
    hi = v.astype(bf16)
    rest = v - hi.astype(f32)
    mid = rest.astype(bf16)
    lo = (rest - mid.astype(f32)).astype(bf16)
    return hi, mid, lo


def lane_pack(v):
    lane = lax.broadcasted_iota(jnp.int32, v.shape, 1)
    hi, mid, lo = (part.astype(f32) for part in split3(v))
    packed = jnp.where(lane < 16, hi, jnp.where(lane < 32, mid, jnp.where(lane < 48, lo, 0.0)))
    return packed.astype(bf16)


def dot(a, b, ca=1, cb=0):
    return lax.dot_general(a, b, (((ca,), (cb,)), ((), ())), preferred_element_type=f32)


def in_hbm(v):
    return pltpu.with_memory_space_constraint(v, pltpu.HBM)


def pack_body(first, x_ref, out_ref, held, in_sems, out_sems):
    count = held.shape[0]
    loads = [pltpu.make_async_copy(x_ref.at[first + s], held.at[s], in_sems.at[s]) for s in range(count)]
    for load in loads:
        load.start()
    stores = []
    for s in range(count):
        loads[s].wait()
        for g in range(GROUPS):
            pieces = (
                (g * GROUP_X, 0, GROUP_X),
                (INNER + g * STATE, GROUP_X, STATE),
                (INNER + (GROUPS + g) * STATE, GROUP_X + STATE, STATE),
            )
            for i, (src, dst, width) in enumerate(pieces):
                store = pltpu.make_async_copy(
                    held.at[s, :, pl.ds(src, width)],
                    out_ref.at[g, s, :, pl.ds(dst, width)],
                    out_sems.at[s, g, i],
                )
                store.start()
                stores.append(store)
    for store in stores:
        store.wait()


def pack_groups(conv_input, first, count):
    return pl.pallas_call(
        functools.partial(pack_body, first),
        in_specs=[pl.BlockSpec(memory_space=pl.ANY)],
        out_specs=pl.BlockSpec(memory_space=pl.ANY),
        out_shape=pltpu.HBM((GROUPS, count, ROWS, GROUP_CH), bf16),
        scratch_shapes=[
            pltpu.VMEM((count,) + conv_input.shape[1:], bf16),
            pltpu.SemaphoreType.DMA((count,)),
            pltpu.SemaphoreType.DMA((count, GROUPS, 3)),
        ],
        compiler_params=params(12),
        name="pack_groups",
    )(in_hbm(conv_input))


def front_body(j_ref, bias_ref, rate_ref, skip_ref, dt_ref, out_ref):
    row = lax.broadcasted_iota(jnp.int32, (EXT, 128), 0)
    lane = lax.broadcasted_iota(jnp.int32, (EXT, 128), 1)
    even = (lane & 1) == 0
    values = jnp.where(even, skip_ref[0], skip_ref[1])
    values = jnp.where(row == 0, jnp.where(even, bias_ref[0], bias_ref[1]), values)
    values = jnp.where(row == 1, jnp.where(even, rate_ref[0], rate_ref[1]), values)
    here = ((lane & 15) >> 1 == j_ref[0]) & (row < 3)
    packed = lane_pack(jnp.where(here, values, 0.0))
    rows = dt_ref.shape[0]
    for g in range(GROUPS):
        out_ref[g, 0:rows, :] = dt_ref[...]
        out_ref[g, rows : rows + EXT, :] = packed


def front_rows(j, dt_bias, decay_rate, skip_d, dt_rows):
    scalar = pl.BlockSpec(memory_space=pltpu.SMEM)
    return pl.pallas_call(
        front_body,
        in_specs=[scalar, scalar, scalar, scalar, pl.BlockSpec(memory_space=pltpu.VMEM)],
        out_specs=pl.BlockSpec(memory_space=pltpu.VMEM),
        out_shape=pltpu.HBM((GROUPS, dt_rows.shape[0] + EXT, 128), bf16),
        compiler_params=params(8),
        name="front_rows",
    )(j.reshape(1), in_hbm(dt_bias), in_hbm(decay_rate), in_hbm(skip_d), in_hbm(dt_rows))


def steps_body(meta_ref, dt_ref, par_ref, ein_ref, eout_ref, rows_ref):
    s = pl.program_id(0)
    z, j, length = meta_ref[0], meta_ref[1], meta_ref[2 + s]
    src = lax.broadcasted_iota(jnp.int32, (128, 128), 0)
    dst = lax.broadcasted_iota(jnp.int32, (128, 128), 1)
    join = ((src & 15) == (dst & 15)) & (src < 48) & (dst < 48)
    par = jnp.sum(par_ref[...].astype(f32), axis=0).astype(bf16)
    par = dot(par, join.astype(f32).astype(bf16))
    bias, rate, skip = par[0:1], par[1:2], par[2:3]
    sel = ((src == j * GROUP_HEADS + (dst & 15)) & (dst < 48)).astype(f32).astype(bf16)
    raw = dot(dt_ref[...].reshape(SLAB, 128), sel)
    pos = z * SLAB + lax.broadcasted_iota(jnp.int32, (SLAB, 128), 0)
    arg = raw + bias
    dt = jnp.maximum(arg, 0.0) + jnp.log1p(jnp.exp(-jnp.abs(arg)))
    dt = jnp.where(pos < length, dt, 0.0)
    rise = -rate * dt
    row = lax.broadcasted_iota(jnp.int32, (SLAB, SLAB), 0)
    col = lax.broadcasted_iota(jnp.int32, (SLAB, SLAB), 1)
    tri = (row >= col).astype(f32).astype(bf16)
    hi, mid, lo = split3(rise)
    cum = dot(tri, hi) + dot(tri, mid) + dot(tri, lo)
    middle = 0.5 * cum[SLAB - 1 : SLAB]
    ein_ref[0] = lane_pack(jnp.exp(middle - cum) * dt)
    eout_ref[0] = lane_pack(jnp.exp(cum - middle))
    which = lax.broadcasted_iota(jnp.int32, (EXT, 128), 0)
    rows_ref[0] = lane_pack(jnp.where(which == 0, jnp.exp(middle), skip) + jnp.zeros((EXT, 128), f32))


def step_factors(meta, dt_all, par_all, seqs):
    return pl.pallas_call(
        steps_body,
        grid_spec=pltpu.PrefetchScalarGridSpec(
            num_scalar_prefetch=1,
            grid=(seqs,),
            in_specs=[
                pl.BlockSpec((GROUPS, ROWS, 128), lambda s, m: (0, s, 0)),
                pl.BlockSpec((GROUPS, EXT, 128), lambda s, m: (0, 0, 0)),
            ],
            out_specs=[
                pl.BlockSpec((1, SLAB, 128), lambda s, m: (s, 0, 0)),
                pl.BlockSpec((1, SLAB, 128), lambda s, m: (s, 0, 0)),
                pl.BlockSpec((1, EXT, 128), lambda s, m: (s, 0, 0)),
            ],
        ),
        out_shape=[
            jax.ShapeDtypeStruct((seqs, SLAB, 128), bf16),
            jax.ShapeDtypeStruct((seqs, SLAB, 128), bf16),
            jax.ShapeDtypeStruct((seqs, EXT, 128), bf16),
        ],
        compiler_params=params(16),
        name="step_factors",
    )(meta, dt_all, par_all)


def conv_rows(w_ref, lane, win):
    acc = w_ref[3:4, lane : lane + 256] * win[8:]
    for back in (1, 2, 3):
        acc = acc + w_ref[3 - back : 4 - back, lane : lane + 256] * pltpu.roll(win, back, 0)[8:]
    return acc + acc * jnp.tanh(acc)


def conv_body(first, meta_ref, recv_ref, w_ref, xbc_ref, xs):
    s = pl.program_id(0)
    z, length = meta_ref[0], meta_ref[2 + first + s]
    xs[0:8, :] = jnp.zeros((8, GROUP_CH), f32)
    for b in range(GROUPS):
        xs[8 + ROWS * b : 8 + ROWS * (b + 1), :] = recv_ref[b, 0].astype(f32)

    def per_rows(b, _):
        start = pl.multiple_of(b * ROWS, ROWS)
        pos = z * SLAB + start + lax.broadcasted_iota(jnp.int32, (ROWS, 256), 0)
        keep = pos < length
        for lane in range(0, GROUP_CH, 256):
            rows = conv_rows(w_ref, lane, xs[pl.ds(start, ROWS + 8), lane : lane + 256])
            xbc_ref[0, pl.ds(start, ROWS), lane : lane + 256] = jnp.where(keep, rows, 0.0).astype(bf16)
        return 0

    lax.fori_loop(0, GROUPS, per_rows, 0)


def conv_slab(meta, recv, weight, first, count):
    return pl.pallas_call(
        functools.partial(conv_body, first),
        grid_spec=pltpu.PrefetchScalarGridSpec(
            num_scalar_prefetch=1,
            grid=(count,),
            in_specs=[
                pl.BlockSpec((GROUPS, 1, ROWS, GROUP_CH), lambda s, m: (0, s, 0, 0)),
                pl.BlockSpec((4, GROUP_CH), lambda s, m: (0, 0)),
            ],
            out_specs=pl.BlockSpec((1, SLAB, GROUP_CH), lambda s, m: (s, 0, 0)),
            scratch_shapes=[pltpu.VMEM((SLAB + 8, GROUP_CH), f32)],
        ),
        out_shape=pltpu.HBM((count, SLAB, GROUP_CH), bf16),
        compiler_params=params(24),
        name="conv_slab",
    )(meta, in_hbm(recv), weight)


def edge_body(first, meta_ref, xbc_ref, raw_ref, halo_ref, w_ref, ein_ref, rows_ref, e3_ref, edge_ref, sout_ref, scaled):
    s = pl.program_id(0)
    z, length = meta_ref[0], meta_ref[2 + first + s]
    keep = z * SLAB + lax.broadcasted_iota(jnp.int32, (EXT, 256), 0) < length
    for lane in range(0, GROUP_CH, 256):
        lanes = slice(lane, lane + 256)
        win = jnp.concatenate([halo_ref[0, :, lanes], raw_ref[0, 0, :, lanes].astype(f32)], axis=0)
        edge_ref[0, :, lanes] = jnp.where(keep, conv_rows(w_ref, lane, win), 0.0).astype(bf16)
    e3 = e3_ref[...]
    for b in range(0, SLAB, 128):
        here = slice(b, b + 128)
        x = xbc_ref[0, here, 0:GROUP_X]
        if b == 0:
            x = jnp.concatenate([edge_ref[0, :, 0:GROUP_X], x[EXT:]], axis=0)
        scaled[here] = (x.astype(f32) * dot(ein_ref[0, here], e3)).astype(bf16)
    b_lanes = slice(GROUP_X, GROUP_X + STATE)
    b_all = jnp.concatenate([edge_ref[0, :, b_lanes], xbc_ref[0, EXT:, b_lanes]], axis=0)
    state = dot(b_all, scaled[...], 0, 0)
    grow = dot(rows_ref[0], e3)[0:1]
    state = (state * grow).astype(bf16)
    which = lax.broadcasted_iota(jnp.int32, (EXT, GROUP_X), 0)
    hi, mid, lo = (part.astype(f32) for part in split3(grow))
    extra = jnp.where(which == 0, hi, jnp.where(which == 1, mid, jnp.where(which == 2, lo, 0.0))).astype(bf16)
    for k in range(GROUPS):
        sout_ref[k, 0, 0:STATE, :] = state[:, 128 * k : 128 * (k + 1)]
        sout_ref[k, 0, STATE : STATE + EXT, :] = extra[:, 128 * k : 128 * (k + 1)]


def edge_and_state(meta, xbc, recv, halo, weight, ein, rows, e3, first, count):
    return pl.pallas_call(
        functools.partial(edge_body, first),
        grid_spec=pltpu.PrefetchScalarGridSpec(
            num_scalar_prefetch=1,
            grid=(count,),
            in_specs=[
                pl.BlockSpec((1, SLAB, GROUP_CH), lambda s, m: (s, 0, 0)),
                pl.BlockSpec((1, 1, EXT, GROUP_CH), lambda s, m: (0, s, 0, 0)),
                pl.BlockSpec((1, 8, GROUP_CH), lambda s, m: (s, 0, 0)),
                pl.BlockSpec((4, GROUP_CH), lambda s, m: (0, 0)),
                pl.BlockSpec((1, SLAB, 128), lambda s, m: (first + s, 0, 0)),
                pl.BlockSpec((1, EXT, 128), lambda s, m: (first + s, 0, 0)),
                pl.BlockSpec((128, GROUP_X), lambda s, m: (0, 0)),
            ],
            out_specs=[
                pl.BlockSpec((1, EXT, GROUP_CH), lambda s, m: (s, 0, 0)),
                pl.BlockSpec((GROUPS, 1, STATE + EXT, 128), lambda s, m: (0, s, 0, 0)),
            ],
            scratch_shapes=[pltpu.VMEM((SLAB, GROUP_X), bf16)],
        ),
        out_shape=[
            pltpu.HBM((count, SLAB, GROUP_CH), bf16),
            pltpu.HBM((GROUPS, count, STATE + EXT, 128), bf16),
        ],
        input_output_aliases={1: 0},
        compiler_params=params(24),
        name="edge_and_state",
    )(meta, in_hbm(xbc), in_hbm(recv), halo, weight, ein, rows, e3)


def inner_body(xbc_ref, ein_ref, eout_ref, rows_ref, e3_ref, out_ref):
    e3 = e3_ref[...]
    x = xbc_ref[0, :, 0:GROUP_X]
    scaled = (x.astype(f32) * dot(ein_ref[0], e3)).astype(bf16)
    skip = dot(rows_ref[0], e3)[1:2]
    half = SLAB // 2
    for part in range(2):
        rows = slice(part * half, (part + 1) * half)
        upto = (part + 1) * half
        c_part = xbc_ref[0, rows, GROUP_X + STATE : GROUP_CH]
        b_part = xbc_ref[0, 0:upto, GROUP_X : GROUP_X + STATE]
        scores = dot(c_part, b_part, 1, 1)
        t_at = part * half + lax.broadcasted_iota(jnp.int32, (half, upto), 0)
        u_at = lax.broadcasted_iota(jnp.int32, (half, upto), 1)
        scores = jnp.where(u_at <= t_at, scores, 0.0).astype(bf16)
        acc = dot(scores, scaled[0:upto])
        out_ref[0, rows, :] = dot(eout_ref[0, rows, :], e3) * acc + skip * x[rows].astype(f32)


def inner_output(xbc, ein, eout, rows, e3, first, count):
    return pl.pallas_call(
        inner_body,
        grid=(count,),
        in_specs=[
            pl.BlockSpec((1, SLAB, GROUP_CH), lambda s: (s, 0, 0)),
            pl.BlockSpec((1, SLAB, 128), lambda s: (first + s, 0, 0)),
            pl.BlockSpec((1, SLAB, 128), lambda s: (first + s, 0, 0)),
            pl.BlockSpec((1, EXT, 128), lambda s: (first + s, 0, 0)),
            pl.BlockSpec((128, GROUP_X), lambda s: (0, 0)),
        ],
        out_specs=pl.BlockSpec((1, SLAB, GROUP_X), lambda s: (s, 0, 0)),
        out_shape=pltpu.HBM((count, SLAB, GROUP_X), f32),
        compiler_params=params(24),
        name="inner_output",
    )(in_hbm(xbc), ein, eout, rows, e3)


def scan_body(got_ref, seed_ref, start_ref, final_ref):
    state = seed_ref[0].astype(f32).T
    for k in range(got_ref.shape[0]):
        start_ref[k, 0] = state.astype(bf16)
        extra = got_ref[k, 0, STATE : STATE + EXT, :].astype(f32)
        root = extra[0:1] + extra[1:2] + extra[2:3]
        state = (root * root) * state + got_ref[k, 0, 0:STATE, :].astype(f32)
    final_ref[0] = state.T.astype(bf16)


def scan_slabs(got, seed, first, count):
    slabs = got.shape[0]
    return pl.pallas_call(
        scan_body,
        grid=(count,),
        in_specs=[
            pl.BlockSpec((slabs, 1, STATE + EXT, 128), lambda s: (0, s, 0, 0)),
            pl.BlockSpec((1, 128, STATE), lambda s: (first + s, 0, 0)),
        ],
        out_specs=[
            pl.BlockSpec((slabs, 1, STATE, 128), lambda s: (0, s, 0, 0)),
            pl.BlockSpec((1, 128, STATE), lambda s: (s, 0, 0)),
        ],
        out_shape=[
            pltpu.HBM((slabs, count, STATE, 128), bf16),
            jax.ShapeDtypeStruct((count, 128, STATE), bf16),
        ],
        compiler_params=params(12),
        name="scan_slabs",
    )(got, seed)


def finish_body(part_ref, c_ref, start_ref, eout_ref, rows_ref, e3_ref, out_ref):
    e3 = e3_ref[...]
    grow = dot(rows_ref[0], e3)[0:1]
    state = jnp.concatenate([start_ref[k, 0] for k in range(GROUPS)], axis=1)
    for b in range(out_ref.shape[0]):
        here = slice(ROWS * b, ROWS * (b + 1))
        carried = dot(c_ref[0, here], state)
        out_ref[b, 0] = (part_ref[0, here] + dot(eout_ref[0, here], e3) * (grow * carried)).astype(bf16)


def finish_output(part, xbc, start, eout, rows, e3, first, count):
    c_at = GROUP_CH // STATE - 1
    half = SLAB // 2
    return pl.pallas_call(
        finish_body,
        grid=(count, 2),
        in_specs=[
            pl.BlockSpec((1, half, GROUP_X), lambda s, h: (s, h, 0)),
            pl.BlockSpec((1, half, STATE), lambda s, h: (s, h, c_at)),
            pl.BlockSpec((GROUPS, 1, STATE, 128), lambda s, h: (0, s, 0, 0)),
            pl.BlockSpec((1, half, 128), lambda s, h: (first + s, h, 0)),
            pl.BlockSpec((1, EXT, 128), lambda s, h: (first + s, 0, 0)),
            pl.BlockSpec((128, GROUP_X), lambda s, h: (0, 0)),
        ],
        out_specs=pl.BlockSpec((GROUPS // 2, 1, ROWS, GROUP_X), lambda s, h: (h, s, 0, 0)),
        out_shape=pltpu.HBM((GROUPS, count, ROWS, GROUP_X), bf16),
        compiler_params=params(24),
        name="finish_output",
    )(in_hbm(part), in_hbm(xbc), start, eout, rows, e3)


PAIR = 2


def norm_body(meta_ref, y_ref, gate_ref, gain_ref, out_ref):
    at = (meta_ref[0] * GROUPS + meta_ref[1]) * ROWS
    step = 32
    for q in range(PAIR):
        lanes = slice(GROUP_X * q, GROUP_X * (q + 1))
        gain = gain_ref[:, lanes]
        for s in range(out_ref.shape[0]):
            for row in range(0, ROWS, step):
                here = slice(row, row + step)
                gated = y_ref[q, s, here].astype(f32) * silu(gate_ref[s, here, lanes].astype(f32))
                mean = jnp.mean(gated * gated, axis=-1, keepdims=True)
                pos = at + row + lax.broadcasted_iota(jnp.int32, (step, 1), 0)
                scale = jnp.where(pos < meta_ref[2 + s], lax.rsqrt(mean + norm_eps), 0.0)
                out_ref[s, here, lanes] = (gated * scale * gain).astype(bf16)


def gated_norm(meta, y, gate_z, gain, seqs):
    width = PAIR * GROUP_X
    return pl.pallas_call(
        norm_body,
        grid_spec=pltpu.PrefetchScalarGridSpec(
            num_scalar_prefetch=1,
            grid=(GROUPS // PAIR,),
            in_specs=[
                pl.BlockSpec((PAIR, seqs, ROWS, GROUP_X), lambda g, m: (g, 0, 0, 0)),
                pl.BlockSpec((seqs, ROWS, width), lambda g, m: (0, 0, g)),
                pl.BlockSpec((1, width), lambda g, m: (0, g)),
            ],
            out_specs=pl.BlockSpec((seqs, ROWS, width), lambda g, m: (0, 0, g)),
        ),
        out_shape=pltpu.HBM((seqs, ROWS, INNER), bf16),
        compiler_params=params(20),
        name="gated_norm",
    )(meta, in_hbm(y), gate_z, gain)


def local(
    conv_input,
    dt_raw,
    gate_z,
    conv_weight,
    dt_bias,
    decay_rate,
    skip_d,
    norm_gain,
    pool_state,
    pool_tail,
    route_owner,
    route_slot,
    prefix_hit,
    lengths,
):
    seqs = conv_input.shape[0]
    slabs = lax.axis_size("z")
    z = lax.axis_index("z")
    j = lax.axis_index("j")
    first_seq = lax.axis_index("pool") * seqs
    slot_count = pool_state.shape[0]
    flip = [(a * GROUPS + b, b * GROUPS + a) for a in range(slabs) for b in range(GROUPS)]

    def group_columns(source):
        last = source.ndim - 1
        return jnp.concatenate(
            [
                lax.dynamic_slice_in_dim(source, j * GROUP_X, GROUP_X, last),
                lax.dynamic_slice_in_dim(source, INNER + j * STATE, STATE, last),
                lax.dynamic_slice_in_dim(source, INNER + (GROUPS + j) * STATE, STATE, last),
            ],
            axis=-1,
        )

    front = front_rows(j, dt_bias, decay_rate, skip_d, dt_raw.reshape(seqs * ROWS, 128))
    front = lax.all_to_all(front, "j", 0, 0, tiled=True)
    sent = pack_groups(conv_input, 0, seqs)
    sent, front = lax.optimization_barrier((sent, front))
    recv = lax.all_to_all(sent, "j", 0, 0, tiled=True)

    valid_len = lax.dynamic_slice_in_dim(lengths, first_seq, seqs)
    hit = lax.dynamic_slice_in_dim(prefix_hit, first_seq, seqs)
    owner = lax.dynamic_slice_in_dim(route_owner, first_seq, seqs)
    slot = lax.dynamic_slice_in_dim(route_slot, first_seq, seqs)
    meta = jnp.concatenate([jnp.stack([z, j]).astype(jnp.int32), valid_len])

    pools = lax.axis_size("pool")

    def from_pools(mine):
        parts = [mine]
        for k in range(1, pools):
            parts.append(lax.ppermute(mine, "pool", [(i, (i + k) % pools) for i in range(pools)]))
        return jnp.concatenate(parts, axis=0)

    par_all = lax.ppermute(front[:, seqs * ROWS :], ("z", "j"), flip)
    mine, par_all = lax.optimization_barrier((pool_state.reshape(slot_count, 128, STATE), par_all))
    pick = (lax.axis_index("pool") - owner) % pools * slot_count + slot
    seed = jnp.take(from_pools(mine), pick, axis=0) * hit.astype(bf16)[:, None, None]
    ein, eout, rows = step_factors(meta, front, par_all, seqs)
    tails, seed, ein = lax.optimization_barrier((group_columns(pool_tail), seed, ein))
    seed = lax.ppermute(seed, ("z", "j"), flip)
    tail = jnp.take(from_pools(tails), pick, axis=0) * hit.astype(bf16)[:, None, None]

    head_of = jnp.arange(GROUP_X, dtype=jnp.int32)[None, :] // HEAD_DIM
    src = jnp.arange(128, dtype=jnp.int32)[:, None]
    e3 = ((src < 48) & ((src & 15) == head_of)).astype(bf16)
    weight = 0.5 * group_columns(conv_weight)

    before = lax.ppermute(recv[GROUPS - 1, :, ROWS - 3 :], "z", [(k, k + 1) for k in range(slabs - 1)])
    halo = jnp.where(z == 0, tail, before).astype(f32)
    halo = jnp.pad(halo, ((0, 0), (5, 0), (0, 0)))

    xbc = conv_slab(meta, recv, weight, 0, seqs)
    xbc, sout = edge_and_state(meta, xbc, recv, halo, weight, ein, rows, e3, 0, seqs)
    sout, seed = lax.optimization_barrier((sout, seed))
    got = lax.all_to_all(sout, "z", 0, 0, tiled=True)
    part = inner_output(xbc, ein, eout, rows, e3, 0, seqs)
    start, final = scan_slabs(got, seed, 0, seqs)
    back = lax.all_to_all(start, "z", 0, 0, tiled=True)
    final = lax.ppermute(final, ("z", "j"), flip)
    y = finish_output(part, xbc, back, eout, rows, e3, 0, seqs)
    token = lax.all_to_all(y, "j", 0, 0, tiled=True)
    mixed = gated_norm(meta, token, gate_z, norm_gain.reshape(1, INNER), seqs)
    return (mixed, final.astype(f32).reshape(seqs, 2, HEAD_DIM, STATE))


def solution(mesh):
    seq_count, pool_count = mesh.devices.shape
    split = Mesh(mesh.devices.reshape(seq_count // GROUPS, GROUPS, pool_count), ("z", "j", "pool"))
    seq = ("z", "j")
    in_specs = (
        P("pool", seq, None),
        P("pool", seq, None),
        P("pool", seq, None),
        P(),
        P(seq),
        P(seq),
        P(seq),
        P(),
        P("pool", seq, None, None),
        P("pool", None, None),
        P(),
        P(),
        P(),
        P(),
    )
    out_specs = (P("pool", seq, None), P("pool", seq, None, None))
    return jax.shard_map(local, mesh=split, in_specs=in_specs, out_specs=out_specs, check_vma=False)
```
